32 devices in a mesh: wide: 16 (over z, y, core), narrow: 2 (over x).
Axes of the slice: x: 2, y: 2, z: 4, core: 2. Of those that a mesh axis runs over, the one named last changes fastest.
Arguments:
- tokens: bfloat16 [16384, 768], P(('wide', 'narrow')), may hold values from -6 to 6
- qkv_weight: bfloat16 [768, 2304], P('wide'), may hold values from -0.21875 to 0.21875
- qv_bias: bfloat16 [2, 768], P(None, 'wide'), may hold values from -3 to 3
- proj_weight: bfloat16 [768, 768], P('wide'), may hold values from -1.75 to 1.75
- proj_bias: bfloat16 [768], P('wide'), may hold values from -3 to 3
- fc1_weight: bfloat16 [768, 3072], P('wide'), may hold values from -0.21875 to 0.21875
- fc1_bias: bfloat16 [3072], P('wide'), may hold values from -3 to 3
- fc2_weight: bfloat16 [3072, 768], P('wide'), may hold values from -0.109375 to 0.109375
- fc2_bias: bfloat16 [768], P('wide'), may hold values from -3 to 3
- norm1_gain: bfloat16 [768], P('wide'), may hold values from 0.5 to 1.5
- norm1_shift: bfloat16 [768], P('wide'), may hold values from -2 to 2
- norm2_gain: bfloat16 [768], P('wide'), may hold values from 0.5 to 1.5
- norm2_shift: bfloat16 [768], P('wide'), may hold values from -2 to 2
- segment_ids: int32 [16384], P(('wide', 'narrow')), may hold values from 0 to 6, as said below
- key_mask: int32 [16384], P(('wide', 'narrow')), may hold values from 0 to 1, as said below
- positions: int32 [16384], P(('wide', 'narrow')), may hold values from 0 to 3139, as said below
- cotangent: bfloat16 [16384, 768], P(('wide', 'narrow')), may hold values from -6 to 6
Outputs:
- block_out: bfloat16 [16384, 768], P(('wide', 'narrow'))
- grad_tokens: float32 [16384, 768], P(('wide', 'narrow'))
- grad_qkv_weight: float32 [768, 2304], P('wide')
- grad_qv_bias: float32 [2, 768], P(None, 'wide')
- grad_proj_weight: float32 [768, 768], P('wide')
- grad_proj_bias: float32 [768], P('wide')
- grad_fc1_weight: float32 [768, 3072], P('wide')
- grad_fc1_bias: float32 [3072], P('wide')
- grad_fc2_weight: float32 [3072, 768], P('wide')
- grad_fc2_bias: float32 [768], P('wide')
- grad_norm1_gain: float32 [768], P('wide')
- grad_norm1_shift: float32 [768], P('wide')
- grad_norm2_gain: float32 [768], P('wide')
- grad_norm2_shift: float32 [768], P('wide')
The draws below stay inside these ranges and needn't reach their ends.
Inputs may be any that keep to these rules, and one draw needn't show every extreme that they name: `segment_ids`: each block of 512 rows holds whole clips of 79, 157 or 314 tokens laid end to end from its first row, numbered 0, 1, 2 and so on within the block; the rows after the last clip are padding and carry the next number. `key_mask`: 1 on the rows of clips, 0 on padding rows. `positions`: below 10 times the length of the token's clip; 0 on padding rows.
All inputs are finite; a program needn't handle non-finite values.
Results may differ from the reference program's by a relative error of at most 0.008.
Values may be sent and summed in bfloat16 or wider, within the bound.
No kernel may reach another device: no remote copies, remote signals or barrier semaphores. Data moves between devices by JAX's collectives and lax.ppermute only.
A program may use at most 192 MiB of HBM per device.

```python
import math
import jax
import jax.numpy as jnp
from jax import lax

D = 768
FF = 3072
HEAD = 64
HEADS = 12
CLIP_S = 79
CLIP_M = 157
CLIP_L = 314
TOK_DEV = 512
TOKENS = 16384


def pack(key):
    block_count = TOKENS // TOK_DEV
    clip_slots = TOK_DEV // CLIP_S + 1
    base_key = jax.random.fold_in(key, 7)
    draw_kind = jax.random.randint(jax.random.fold_in(base_key, 1), (block_count, clip_slots), 0, 10)
    block_row = jnp.arange(block_count, dtype=jnp.int32)[:, None]
    slot_col = jnp.arange(clip_slots, dtype=jnp.int32)[None, :]
    draw_kind = jnp.where(block_row == 0, 0, draw_kind)
    draw_kind = jnp.where((block_row == 1) & (slot_col == 0), 9, draw_kind)
    clip_sizes = jnp.where(draw_kind < 6, CLIP_S, jnp.where(draw_kind < 9, CLIP_M, CLIP_L)).astype(jnp.int32)
    clip_ends = jnp.cumsum(clip_sizes, axis=1)
    fitting = clip_ends <= TOK_DEV
    slot_index = jnp.arange(TOK_DEV, dtype=jnp.int32)
    passed = (clip_ends[:, None, :] <= slot_index[None, :, None]) & fitting[:, None, :]
    segment = jnp.sum(passed.astype(jnp.int32), axis=2)
    used_rows = jnp.sum(jnp.where(fitting, clip_sizes, 0), axis=1)
    valid_rows = (slot_index[None, :] < used_rows[:, None]).astype(jnp.int32)
    slot_ids = jnp.arange(clip_slots, dtype=jnp.int32)
    own_clip = segment[:, :, None] == slot_ids[None, None, :]
    own_size = jnp.sum(jnp.where(own_clip, clip_sizes[:, None, :], 0), axis=2)
    own_end = jnp.sum(jnp.where(own_clip, clip_ends[:, None, :], 0), axis=2)
    grid_size = jnp.maximum(10 * own_size, 1)
    places = jax.random.randint(jax.random.fold_in(base_key, 2), (block_count, TOK_DEV), 0, grid_size)
    last_row = slot_index[None, :] + 1 == own_end
    places = jnp.where(last_row, grid_size - 1, places)
    places = jnp.where(valid_rows == 1, places, 0)
    return (segment.reshape(-1).astype(jnp.int32), valid_rows.reshape(-1).astype(jnp.int32), places.reshape(-1).astype(jnp.int32))


def draw_segment_ids(key, part):
    return pack(key)[0]


def draw_key_mask(key, part):
    return pack(key)[1]


def draw_positions(key, part):
    return pack(key)[2]


def level_of(rng, dims, pieces, smallest, high):
    def one(dim, shards_of):
        draws = jax.random.uniform(jax.random.fold_in(jax.random.fold_in(rng, 6), dim), (shards_of,), jnp.float32, smallest / len(pieces), high / len(pieces))
        return jnp.repeat(jnp.exp(draws), dims[dim] // shards_of).reshape((-1,) + (1,) * (len(dims) - dim - 1))

    factor_of = one(*pieces[0])
    for cut in pieces[1:]:
        factor_of = factor_of * one(*cut)
    return factor_of


def normal_values(own_key, shape, deviation, limit, cuts=(), held_as=jnp.bfloat16):
    array = jax.random.normal(own_key, shape, jnp.float32) * deviation
    if len(cuts) > 0:
        array = level_of(own_key, shape, cuts, -0.22, 0.18) * array
    return jnp.clip(array, min=-limit, max=limit).astype(held_as)


def setup_inputs(seed: int = 0) -> dict:
    arg_keys = jax.random.split(jax.random.key(seed), 18)
    return {
        "tokens": normal_values(arg_keys[0], (TOKENS, D), 1.0, 6.0, ((0, 32),)),
        "qkv_weight": normal_values(arg_keys[1], (D, 3 * D), D ** -0.5, 0.21875, ((0, 16),)),
        "qv_bias": normal_values(arg_keys[2], (2, D), 0.5, 3.0, ((1, 16),)),
        "proj_weight": normal_values(arg_keys[3], (D, D), (D // 64) ** -0.5, 1.75, ((0, 16),)),
        "proj_bias": normal_values(arg_keys[4], (D,), 0.5, 3.0, ((0, 16),)),
        "fc1_weight": normal_values(arg_keys[5], (D, FF), D ** -0.5, 0.21875, ((0, 16),)),
        "fc1_bias": normal_values(arg_keys[6], (FF,), 0.5, 3.0, ((0, 16),)),
        "fc2_weight": normal_values(arg_keys[7], (FF, D), FF ** -0.5, 0.109375, ((0, 16),)),
        "fc2_bias": normal_values(arg_keys[8], (D,), 0.5, 3.0, ((0, 16),)),
        "norm1_gain": jnp.clip(1.0 + 0.1 * jax.random.normal(arg_keys[9], (D,), jnp.float32), 0.5, 1.5).astype(jnp.bfloat16),
        "norm1_shift": normal_values(arg_keys[10], (D,), 0.3, 2.0, ((0, 16),)),
        "norm2_gain": jnp.clip(1.0 + 0.1 * jax.random.normal(arg_keys[11], (D,), jnp.float32), 0.5, 1.5).astype(jnp.bfloat16),
        "norm2_shift": normal_values(arg_keys[12], (D,), 0.3, 2.0, ((0, 16),)),
        "segment_ids": draw_segment_ids(jax.random.fold_in(arg_keys[17], 71), 0),
        "key_mask": draw_key_mask(jax.random.fold_in(arg_keys[17], 71), 0),
        "positions": draw_positions(jax.random.fold_in(arg_keys[17], 71), 0),
        "cotangent": normal_values(arg_keys[16], (TOKENS, D), 1.0, 6.0, ((0, 32),)),
    }


@jax.custom_vjp
def low(v):
    return lax.optimization_barrier(v.astype(jnp.bfloat16)).astype(jnp.float32)

@jax.custom_vjp
def low_back(v):
    return v

def low_keep(v):
    return (low(v), None)

def low_pass(kept, grad):
    return (grad,)

def back_keep(v):
    return (v, None)

def back_low(kept, grad):
    return (low(grad),)
low.defvjp(low_keep, low_pass)
low_back.defvjp(back_keep, back_low)
EPSILON = 1e-06
MASKED = -1000000000.0

def matmul_hi(left, right):
    return jnp.dot(left, right, precision=lax.Precision.HIGHEST)

def layer_norm(values, gain, shift):
    average = lax.optimization_barrier(jnp.mean(values, axis=-1, keepdims=True))
    centred = values - average
    variance = lax.optimization_barrier(jnp.mean(centred * centred, axis=-1, keepdims=True))
    return centred * lax.rsqrt(variance + EPSILON) * gain + shift

def position_table(positions):
    column = jnp.arange(D, dtype=jnp.int32)
    frequency = jnp.exp((2 * (column // 2)).astype(jnp.float32) * (-math.log(10000.0) / D))
    angles = positions.astype(jnp.float32)[:, None] * frequency[None, :]
    return jnp.where(column % 2 == 0, jnp.sin(angles), jnp.cos(angles))

def forward(parameters, token_rows, table, allowed):
    qkv_matrix, qv_shift, proj_matrix, proj_shift, up_matrix, up_shift, down_matrix, down_shift, gain_one, shift_one, gain_two, shift_two = parameters
    rows_here = token_rows.shape[0]
    embedded = token_rows + table
    normed1 = low(layer_norm(embedded, gain_one, shift_one))
    qkv_shift = jnp.concatenate([qv_shift[0], jnp.zeros_like(qv_shift[0]), qv_shift[1]])
    projected = low(low_back(matmul_hi(normed1, qkv_matrix) + qkv_shift))
    queries = projected[:, :D].reshape(rows_here, HEADS, HEAD)
    keys_all = projected[:, D:2 * D].reshape(rows_here, HEADS, HEAD)
    values_all = projected[:, 2 * D:].reshape(rows_here, HEADS, HEAD)
    scores = low_back(jnp.einsum('thd,shd->hts', queries, keys_all, precision=lax.Precision.HIGHEST) * HEAD ** (-0.5))
    logits = jnp.where(allowed[None], scores, MASKED)
    row_max = lax.optimization_barrier(jnp.max(logits, axis=-1, keepdims=True))
    exponent = jnp.exp(logits - row_max)
    attn_probs = low(exponent / lax.optimization_barrier(jnp.sum(exponent, axis=-1, keepdims=True)))
    attended = jnp.einsum('hts,shd->thd', attn_probs, values_all, precision=lax.Precision.HIGHEST).reshape(rows_here, D)
    attended = low(low_back(attended))
    branch = low_back(matmul_hi(attended, proj_matrix) + proj_shift)
    middle = embedded + branch
    normed2 = low(layer_norm(middle, gain_two, shift_two))
    pre_act = low_back(matmul_hi(normed2, up_matrix) + up_shift)
    hidden = low(jax.nn.gelu(pre_act, approximate=False))
    return middle + matmul_hi(hidden, down_matrix) + down_shift

def reference(tokens, qkv_weight, qv_bias, proj_weight, proj_bias, fc1_weight, fc1_bias, fc2_weight, fc2_bias, norm1_gain, norm1_shift, norm2_gain, norm2_shift, segment_ids, key_mask, positions, cotangent):
    parameters = tuple((item.astype(jnp.float32) for item in (qkv_weight, qv_bias, proj_weight, proj_bias, fc1_weight, fc1_bias, fc2_weight, fc2_bias, norm1_gain, norm1_shift, norm2_gain, norm2_shift)))
    block_count = tokens.shape[0] // TOK_DEV
    diagonal_ok = jnp.arange(TOK_DEV)[:, None] == jnp.arange(TOK_DEV)[None, :]

    def one_block(running, block_index):
        row_start = (block_index * TOK_DEV).astype(jnp.int32)
        token_rows = lax.dynamic_slice_in_dim(tokens, row_start, TOK_DEV, 0).astype(jnp.float32)
        segments = lax.dynamic_slice_in_dim(segment_ids, row_start, TOK_DEV, 0)
        key_rows = lax.dynamic_slice_in_dim(key_mask, row_start, TOK_DEV, 0)
        place_rows = lax.dynamic_slice_in_dim(positions, row_start, TOK_DEV, 0)
        cotangent_rows = lax.dynamic_slice_in_dim(cotangent, row_start, TOK_DEV, 0).astype(jnp.float32)
        allowed = (segments[:, None] == segments[None, :]) & ((key_rows[None, :] == 1) | diagonal_ok)
        table = position_table(place_rows)
        result_rows, pullback = jax.vjp(lambda params_in, rows_in: forward(params_in, rows_in, table, allowed), parameters, token_rows)
        weight_grads, grad_input = pullback(cotangent_rows)
        running = jax.tree.map(jnp.add, running, weight_grads)
        return (running, (result_rows.astype(jnp.bfloat16), grad_input))
    zero_grads = tuple((jnp.zeros_like(item) for item in parameters))
    totals, (block_outs, grad_inputs) = lax.scan(one_block, zero_grads, jnp.arange(block_count, dtype=jnp.int32))
    return (block_outs.reshape(-1, D), grad_inputs.reshape(-1, D), totals[0], totals[1], totals[2], totals[3], totals[4], totals[5], totals[6], totals[7], totals[8], totals[9], totals[10], totals[11])
```

```python
import math
from functools import partial

import jax
import jax.numpy as jnp
import numpy as np
from jax import lax
from jax.experimental import pallas as pl
from jax.experimental.pallas import tpu as pltpu
from jax.sharding import PartitionSpec as P

D = 768
HEAD = 64
PAIR = 2 * HEAD
EPSILON = 1e-06
MASKED = -1000000000.0
BLOCK = 48
PIECES = 32
AXES = ("wide", "narrow")
F32 = jnp.float32
BF16 = jnp.bfloat16
ROWS = 128


NN = (((1,), (0,)), ((), ()))
NT = (((1,), (1,)), ((), ()))
TN = (((0,), (0,)), ((), ()))


def mm(left, right, dims=NN):
    return lax.dot_general(left, right, dims, preferred_element_type=F32)


def load(own, part, place, weights, sems):
    def one(i, carry):
        pltpu.make_async_copy(own.at[i], weights.at[place(i)], sems.at[0]).start()
        pltpu.make_async_copy(part.at[i], weights.at[place(PIECES + i)], sems.at[1]).start()
        return carry

    lax.fori_loop(0, PIECES, one, 0)


def arrive(own, part, weights, sems):
    pltpu.make_async_copy(own, weights.at[pl.ds(0, PIECES)], sems.at[0]).wait()
    pltpu.make_async_copy(part, weights.at[pl.ds(0, PIECES)], sems.at[1]).wait()


def chunk_of(weights, j):
    return weights[pl.ds(j * (D // BLOCK), D // BLOCK)].reshape(D, D)


def norm_rows(values):
    average = jnp.mean(values, axis=-1, keepdims=True)
    centred = values - average
    variance = jnp.mean(centred * centred, axis=-1, keepdims=True)
    scale = lax.rsqrt(variance + EPSILON)
    return centred * scale, scale


def norm_back(normal, scale, grad, gain):
    scaled = grad * gain
    mean_one = jnp.mean(scaled, axis=-1, keepdims=True)
    mean_two = jnp.mean(scaled * normal, axis=-1, keepdims=True)
    return (scaled - mean_one - normal * mean_two) * scale


def tiles(rows, fn):
    def one(i, carry):
        fn(pl.ds(pl.multiple_of(i * ROWS, ROWS), ROWS))
        return carry

    lax.fori_loop(0, rows // ROWS, one, 0)


def attend_kernel(
    tab, vec, embedded, seg_col, seg_row, key_row, own, part,
    normed1, projected, probs, attended, middle, normed2,
    weights, cap, sems,
):
    step = pl.program_id(0)
    rows = embedded.shape[0]

    @pl.when(step == 0)
    def _():
        load(own, part, lambda i: tab[i], weights, sems)

        def first(rs):
            normal, _ = norm_rows(embedded[rs, :])
            normed1[rs, :] = (normal * vec[4:5, :] + vec[5:6, :]).astype(BF16)
            row = lax.broadcasted_iota(jnp.int32, (ROWS, rows), 0) + rs.start
            col = lax.broadcasted_iota(jnp.int32, (ROWS, rows), 1)
            same = seg_col[rs, :] == seg_row[...]
            seen = (key_row[...] == 1) | (row == col)
            cap[rs, :] = jnp.where(same & seen, -MASKED, MASKED)

        tiles(rows, first)
        arrive(own, part, weights, sems)
        for j in range(3):
            matrix = chunk_of(weights, j)

            def second(rs):
                out = mm(normed1[rs, :], matrix)
                if j == 0:
                    out = out + vec[0:1, :]
                if j == 2:
                    out = out + vec[1:2, :]
                projected[rs, j * D : (j + 1) * D] = out.astype(BF16)

            tiles(rows, second)

    def part_of(base):
        return pl.ds(pl.multiple_of(base * D + step * PAIR, PAIR), PAIR)

    keys = projected[:, part_of(1)]
    values = projected[:, part_of(2)]
    low = lax.broadcasted_iota(jnp.int32, (1, PAIR), 1) < HEAD
    zero = jnp.zeros((), BF16)
    value_two = jnp.concatenate(
        [jnp.where(low, values, zero), jnp.where(low, zero, values)], axis=0
    )

    def third(rs):
        queries = projected[rs, part_of(0)]
        both = []
        for a in range(2):
            mine = jnp.where(low, queries, zero) if a == 0 else jnp.where(low, zero, queries)
            logits = jnp.minimum(mm(mine, keys, NT) * HEAD ** (-0.5), cap[rs, :])
            exponent = jnp.exp(logits - jnp.max(logits, axis=-1, keepdims=True))
            total = jnp.sum(exponent, axis=-1, keepdims=True)
            low_probs = (exponent * (1.0 / total)).astype(BF16)
            probs[a, rs, :] = low_probs
            both.append(low_probs)
        attended[rs, part_of(0)] = mm(jnp.concatenate(both, axis=1), value_two).astype(BF16)

    tiles(rows, third)

    @pl.when(step == pl.num_programs(0) - 1)
    def _():
        matrix = chunk_of(weights, 3)

        def last(rs):
            mid = embedded[rs, :] + (mm(attended[rs, :], matrix) + vec[2:3, :])
            middle[rs, :] = mid
            normal, _ = norm_rows(mid)
            normed2[rs, :] = (normal * vec[6:7, :] + vec[7:8, :]).astype(BF16)

        tiles(rows, last)


def up_kernel(tab, vec, normed2, own, part, hidden, slope, weights, sems):
    step = pl.program_id(0)
    rows = normed2.shape[0]

    @pl.when(step == 0)
    def _():
        load(own, part, lambda i: tab[i], weights, sems)
        arrive(own, part, weights, sems)

    matrix = chunk_of(weights, step)
    shift = vec[pl.ds(8 + step, 1), :]

    def one(rs):
        pre = mm(normed2[rs, :], matrix) + shift
        below = 0.5 + 0.5 * lax.erf(pre * math.sqrt(0.5))
        density = jnp.exp(pre * pre * -0.5) * (1.0 / math.sqrt(2.0 * math.pi))
        hidden[rs, :] = (pre * below).astype(BF16)
        slope[rs, :] = (below + pre * density).astype(BF16)

    tiles(rows, one)


def store_pair(tab, own, send, index, first, second):
    here = tab[160] == 0
    at = tab[128 + index]
    own[at] = jnp.where(here, first, second).astype(BF16)
    send[at] = jnp.where(here, second, first).astype(BF16)


def down_grad_kernel(tab, hidden, cotangent, own, send, total):
    step = pl.program_id(0)
    out = mm(hidden[...], cotangent[...], TN)
    half = out.shape[0] // 2
    for q in range(4):
        first = out[q * BLOCK : (q + 1) * BLOCK]
        second = out[half + q * BLOCK : half + (q + 1) * BLOCK]
        store_pair(tab, own, send, q * 8 + step, first, second)

    @pl.when(step == 0)
    def _():
        total[...] = jnp.sum(cotangent[...].astype(F32), axis=0, keepdims=True)


def down_back_kernel(tab, cotangent, slope, own, part, grad_pre, total, weights, sems):
    step = pl.program_id(0)

    @pl.when(step == 0)
    def _():
        load(own, part, lambda i: tab[64 + i], weights, sems)
        arrive(own, part, weights, sems)

    blocks = slope.shape[1] // BLOCK
    matrix = weights[pl.ds(step * blocks, blocks)].reshape(slope.shape[1], D)
    grad = (mm(cotangent[...], matrix, NT) * slope[...].astype(F32)).astype(BF16)
    grad_pre[...] = grad
    total[...] = jnp.sum(grad.astype(F32), axis=0, keepdims=True)


def wide_grad_kernel(tab, left, right, own, send):
    step = pl.program_id(0)
    out = mm(left[...], right[...], TN)
    for zy in range(8):
        first = out[(2 * zy) * BLOCK : (2 * zy + 1) * BLOCK]
        second = out[(2 * zy + 1) * BLOCK : (2 * zy + 2) * BLOCK]
        store_pair(tab, own, send, step * 8 + zy, first, second)


def qkv_grad_kernel(tab, normed1, attended, grad_projected, grad_branch, own, send):
    step = pl.program_id(0)

    def put(out):
        for zy in range(8):
            first = out[(2 * zy) * BLOCK : (2 * zy + 1) * BLOCK]
            second = out[(2 * zy + 1) * BLOCK : (2 * zy + 2) * BLOCK]
            store_pair(tab, own, send, step * 8 + zy, first, second)

    @pl.when(step < 3)
    def _():
        put(mm(normed1[...], grad_projected[...], TN))

    @pl.when(step == 3)
    def _():
        put(mm(attended[...], grad_branch[...], TN))


def middle_back_kernel(
    tab, vec, grad_pre, middle, cotangent, own2, part2, own1, part1,
    grad_middle, grad_branch, grad_attended, sums,
    weights2, weights1, total, sems,
):
    step = pl.program_id(0)
    rows = middle.shape[0]

    @pl.when(step == 0)
    def _():
        load(own2, part2, lambda i: tab[i], weights2, sems)
        arrive(own2, part2, weights2, sems)
        load(own1, part1, lambda i: tab[i], weights1, sems)

    matrix = chunk_of(weights2, step)

    def one(rs):
        out = mm(grad_pre[rs, :], matrix, NT)
        total[rs, :] = jnp.where(step == 0, out, total[rs, :] + out)

    tiles(rows, one)

    @pl.when(step == pl.num_programs(0) - 1)
    def _():
        arrive(own1, part1, weights1, sems)
        proj = chunk_of(weights1, 3)

        def last(i, carry):
            gain_sum, shift_sum, bias_sum = carry
            rs = pl.ds(pl.multiple_of(i * ROWS, ROWS), ROWS)
            grad = total[rs, :]
            normal, scale = norm_rows(middle[rs, :])
            gain_sum = gain_sum + jnp.sum(grad * normal, axis=0, keepdims=True)
            shift_sum = shift_sum + jnp.sum(grad, axis=0, keepdims=True)
            mid = cotangent[rs, :].astype(F32) + norm_back(normal, scale, grad, vec[6:7, :])
            grad_middle[rs, :] = mid
            branch = mid.astype(BF16)
            grad_branch[rs, :] = branch
            bias_sum = bias_sum + jnp.sum(branch.astype(F32), axis=0, keepdims=True)
            grad_attended[rs, :] = mm(branch, proj, NT).astype(BF16)
            return gain_sum, shift_sum, bias_sum

        zero = jnp.zeros((1, D), F32)
        found = lax.fori_loop(0, rows // ROWS, last, (zero, zero, zero))
        for i in range(3):
            sums[i : i + 1, :] = found[i]


def attend_back_kernel(queries, keys, values, grads, probs, out_q, out_k, out_v, sums, scores):
    rows = queries.shape[0]
    low = lax.broadcasted_iota(jnp.int32, (1, PAIR), 1) < HEAD
    zero = jnp.zeros((), BF16)

    def halves(v):
        return jnp.where(low, v, zero), jnp.where(low, zero, v)

    value_all = values[...]

    def one(rs):
        grad_two = halves(grads[rs, :])
        for a in range(2):
            grad_probs = mm(grad_two[a], value_all, NT)
            prob = probs[a, rs, :].astype(F32)
            product = prob * grad_probs
            inner = jnp.sum(product, axis=-1, keepdims=True)
            scores[a, rs, :] = (product - prob * inner).astype(BF16)

    tiles(rows, one)
    key_two = halves(keys[...])
    query_two = halves(queries[...])
    grad_two = halves(grads[...])
    scale = HEAD ** (-0.5)
    grad_q = (mm(scores[0], key_two[0]) + mm(scores[1], key_two[1])) * scale
    grad_k = (mm(scores[0], query_two[0], TN) + mm(scores[1], query_two[1], TN)) * scale
    grad_v = mm(probs[0], grad_two[0], TN) + mm(probs[1], grad_two[1], TN)
    q = grad_q.astype(BF16)
    v = grad_v.astype(BF16)
    out_q[...] = q
    out_k[...] = grad_k.astype(BF16)
    out_v[...] = v
    sums[0:1, :] = jnp.sum(q.astype(F32), axis=0, keepdims=True)
    sums[1:2, :] = jnp.sum(v.astype(F32), axis=0, keepdims=True)


def first_back_kernel(
    tab, vec, grad_q, grad_k, grad_v, embedded, grad_middle, own, part,
    grad_tokens, sums, weights, sems,
):
    rows = embedded.shape[0]
    load(own, part, lambda i: tab[i], weights, sems)
    arrive(own, part, weights, sems)
    matrices = [chunk_of(weights, j) for j in range(3)]

    def last(i, carry):
        gain_sum, shift_sum = carry
        rs = pl.ds(pl.multiple_of(i * ROWS, ROWS), ROWS)
        grad = (
            mm(grad_q[rs, :], matrices[0], NT)
            + mm(grad_k[rs, :], matrices[1], NT)
            + mm(grad_v[rs, :], matrices[2], NT)
        )
        normal, scale = norm_rows(embedded[rs, :])
        gain_sum = gain_sum + jnp.sum(grad * normal, axis=0, keepdims=True)
        shift_sum = shift_sum + jnp.sum(grad, axis=0, keepdims=True)
        grad_tokens[rs, :] = grad_middle[rs, :] + norm_back(normal, scale, grad, vec[4:5, :])
        return gain_sum, shift_sum

    zero = jnp.zeros((1, D), F32)
    found = lax.fori_loop(0, rows // ROWS, last, (zero, zero))
    for i in range(2):
        sums[i : i + 1, :] = found[i]


def out_kernel(tab, vec, hidden, middle, own, part, block_out, weights, total, sems):
    step = pl.program_id(0)
    rows = middle.shape[0]

    @pl.when(step == 0)
    def _():
        load(own, part, lambda i: tab[64 + i], weights, sems)
        arrive(own, part, weights, sems)

    blocks = hidden.shape[1] // BLOCK
    matrix = weights[pl.ds(step * blocks, blocks)].reshape(hidden.shape[1], D)

    def one(rs):
        out = mm(hidden[rs, :], matrix)
        total[rs, :] = jnp.where(step == 0, out, total[rs, :] + out)

        @pl.when(step == pl.num_programs(0) - 1)
        def _():
            block_out[rs, :] = (middle[rs, :] + total[rs, :] + vec[3:4, :]).astype(BF16)

    tiles(rows, one)


ANY = pl.BlockSpec(memory_space=pl.ANY)


def whole(shape):
    return pl.BlockSpec(shape, lambda i, *_: (0,) * len(shape))


def cols(rows, width, base=0):
    return pl.BlockSpec((rows, width), lambda i, *_: (0, base + i))


def like(shape, dtype):
    return jax.ShapeDtypeStruct(shape, dtype)


def call(kernel, name, grid, ins, outs, scratch, flops, moved, args, tables=1):
    return pl.pallas_call(
        kernel,
        grid_spec=pltpu.PrefetchScalarGridSpec(
            num_scalar_prefetch=tables,
            grid=(grid,),
            in_specs=ins,
            out_specs=[o[0] for o in outs],
            scratch_shapes=scratch,
        ),
        out_shape=[o[1] for o in outs],
        compiler_params=pltpu.CompilerParams(
            dimension_semantics=("arbitrary",), vmem_limit_bytes=56 * 1024 * 1024
        ),
        cost_estimate=pl.CostEstimate(flops=flops, bytes_accessed=moved, transcendentals=0),
        name=name,
    )(*args)


GROUP = pltpu.VMEM((2 * PIECES, BLOCK, D), BF16)
SEMS = pltpu.SemaphoreType.DMA((2,))


def compute(tab, vec_of, tokens, segment_ids, key_mask, positions, cotangent, groups, spread):
    rows = tokens.shape[0]
    hidden_units = 4 * D
    pairs_of_heads = D // PAIR
    embedded = tokens.astype(F32) + position_table(positions)
    square = 2 * rows * D * D
    row_f = (whole((rows, D)), like((rows, D), F32))
    row_b = (whole((rows, D)), like((rows, D), BF16))
    vec = vec_of()
    vec_in = whole(vec.shape)
    own1, part1 = groups(0)
    normed1, projected, probs, attended, middle, normed2 = call(
        attend_kernel, "attend", pairs_of_heads,
        [vec_in, whole((rows, D)), whole((rows, 1)), whole((1, rows)), whole((1, rows)), ANY, ANY],
        [
            row_b,
            (whole((rows, 3 * D)), like((rows, 3 * D), BF16)),
            (
                pl.BlockSpec((2, rows, rows), lambda i, *_: (i, 0, 0)),
                like((2 * pairs_of_heads, rows, rows), BF16),
            ),
            row_b, row_f, row_b,
        ],
        [GROUP, pltpu.VMEM((rows, rows), F32), SEMS],
        8 * square, 20 << 20,
        (
            tab, vec, embedded, segment_ids[:, None], segment_ids[None, :], key_mask[None, :],
            own1, part1,
        ),
    )
    own2, part2 = groups(1)
    wide_b = (cols(rows, D), like((rows, hidden_units), BF16))
    hidden, slope = call(
        up_kernel, "up", 4,
        [vec_in, whole((rows, D)), ANY, ANY], [wide_b, wide_b], [GROUP, SEMS],
        6 * square, 12 << 20, (tab, vec, normed2, own2, part2),
    )
    pieces = (whole((PIECES, BLOCK, D)), like((PIECES, BLOCK, D), BF16))
    step_rows = hidden_units // 8
    own_d, send_d, down_sum = call(
        down_grad_kernel, "down_grad", 8,
        [cols(rows, step_rows), whole((rows, D))],
        [pieces, pieces, (whole((1, D)), like((1, D), F32))], [],
        4 * square, 9 << 20, (tab, hidden, cotangent),
    )
    done_d = spread(2, own_d, send_d)
    own3, part3 = groups(2)
    grad_pre, up_sum = call(
        down_back_kernel, "down_back", 8,
        [whole((rows, D)), cols(rows, step_rows), ANY, ANY],
        [
            (cols(rows, step_rows), like((rows, hidden_units), BF16)),
            (cols(1, step_rows), like((1, hidden_units), F32)),
        ],
        [GROUP, SEMS], 4 * square, 12 << 20, (tab, cotangent, slope, own3, part3),
    )
    own_u, send_u = call(
        wide_grad_kernel, "up_grad", 4,
        [whole((rows, D)), cols(rows, D)], [pieces, pieces], [],
        4 * square, 9 << 20, (tab, normed2, grad_pre),
    )
    done_u = spread(1, own_u, send_u)
    grad_middle, grad_branch, grad_attended, sums_two = call(
        middle_back_kernel, "middle_back", 4,
        [vec_in, cols(rows, D), whole((rows, D)), whole((rows, D)), ANY, ANY, ANY, ANY],
        [row_f, row_b, row_b, (whole((3, D)), like((3, D), F32))],
        [GROUP, GROUP, pltpu.VMEM((rows, D), F32), SEMS],
        5 * square, 20 << 20,
        (tab, vec, grad_pre, middle, cotangent, own2, part2, own1, part1),
    )
    head = lambda base: cols(rows, PAIR, base * pairs_of_heads)
    narrow_b = (cols(rows, PAIR), like((rows, D), BF16))
    grad_q, grad_k, grad_v, sums_qv = call(
        attend_back_kernel, "attend_back", pairs_of_heads,
        [head(0), head(1), head(2), head(0), pl.BlockSpec((2, rows, rows), lambda i, *_: (i, 0, 0))],
        [narrow_b, narrow_b, narrow_b, (cols(2, PAIR), like((2, D), F32))],
        [pltpu.VMEM((2, rows, rows), BF16)],
        8 * square, 12 << 20, (projected, projected, projected, grad_attended, probs), tables=0,
    )
    grad_projected = jnp.concatenate([grad_q, grad_k, grad_v], axis=1)
    own_q, send_q = call(
        qkv_grad_kernel, "qkv_grad", 4,
        [
            whole((rows, D)), whole((rows, D)),
            pl.BlockSpec((rows, D), lambda i, *_: (0, jnp.minimum(i, 2))), whole((rows, D)),
        ],
        [pieces, pieces], [],
        4 * square, 9 << 20, (tab, normed1, attended, grad_projected, grad_branch),
    )
    done_q = spread(0, own_q, send_q)
    grad_tokens, sums_one = call(
        first_back_kernel, "first_back", 1,
        [vec_in] + [whole((rows, D))] * 5 + [ANY, ANY],
        [row_f, (whole((2, D)), like((2, D), F32))], [GROUP, SEMS],
        3 * square, 12 << 20,
        (tab, vec, grad_q, grad_k, grad_v, embedded, grad_middle, own1, part1),
    )
    (block_out,) = call(
        out_kernel, "block_out", 4,
        [vec_in, cols(rows, D), whole((rows, D)), ANY, ANY], [row_b],
        [GROUP, pltpu.VMEM((rows, D), F32), SEMS],
        4 * square, 12 << 20, (tab, vec, hidden, middle, own3, part3),
    )
    small = (
        jnp.concatenate(
            [sums_qv, sums_two[2:3], down_sum, sums_one, sums_two[0:2]], axis=0
        ),
        up_sum,
    )
    return block_out, grad_tokens, done_q, done_u, done_d, small


def position_table(positions):
    column = jnp.arange(D, dtype=jnp.int32)
    frequency = jnp.exp((2 * (column // 2)).astype(F32) * (-math.log(10000.0) / D))
    angles = positions.astype(F32)[:, None] * frequency[None, :]
    return jnp.where(column % 2 == 0, jnp.sin(angles), jnp.cos(angles))


class Ring:
    def __init__(self, shape):
        self.narrow = shape["narrow"]
        self.depth = shape["wide"] // 4

    def move(self, value, fn):
        pairs = []
        for z in range(self.depth):
            for y in range(2):
                for c in range(2):
                    for x in range(self.narrow):
                        u, v, w, t = fn(z, y, c, x)
                        pairs.append(
                            (
                                ((z * 2 + y) * 2 + c) * self.narrow + x,
                                ((u * 2 + v) * 2 + w) * self.narrow + t,
                            )
                        )
        return lax.ppermute(value, AXES, pairs)

    def x(self, value):
        return self.move(value, lambda z, y, c, x: (z, y, c, x ^ 1))

    def y(self, value):
        return self.move(value, lambda z, y, c, x: (z, y ^ 1, c, x))

    def core(self, value):
        return self.move(value, lambda z, y, c, x: (z, y, c ^ 1, x))

    def z(self, value, k):
        return self.move(value, lambda z, y, c, x: ((z + k) % self.depth, y, c, x))

    def gather(self, mine):
        got = [mine] + [self.z(mine, k) for k in range(1, self.depth)]
        one = jnp.stack([g[0] for g in got])
        two = jnp.stack([g[1] for g in got])
        pair_one = jnp.stack([one, self.y(one)])
        pair_two = jnp.stack([two, self.x(two)])
        own = jnp.stack([pair_one, self.x(pair_one), pair_two, self.y(pair_two)])
        return own, self.core(own)

    def scatter(self, own, send):
        own = own.reshape((4, 2, self.depth) + own.shape[1:])
        send = send.reshape(own.shape)
        both = plus(own, self.core(send))
        one = plus(both[0], self.x(both[1]))
        two = plus(both[2], self.y(both[3]))
        one = plus(one[0], self.y(one[1]))
        two = plus(two[0], self.x(two[1]))
        pair = jnp.stack([one, two], axis=1)
        total = pair[0].astype(F32)
        for k in range(1, self.depth):
            total = total + self.z(pair[k], k).astype(F32)
        return total, self.x(total.astype(BF16)).astype(F32)

    def gather_small(self, mine):
        got = jnp.stack([mine] + [self.z(mine, k) for k in range(1, self.depth)])
        got = jnp.stack([got, self.y(got)])
        return jnp.stack([got, self.core(got)]).reshape(4 * self.depth, -1)

    def scatter_small(self, parts):
        parts = parts.reshape(2, 2, self.depth, -1)
        parts = parts[0] + self.core(parts[1])
        parts = parts[0] + self.y(parts[1])
        total = parts[0]
        for k in range(1, self.depth):
            total = total + self.z(parts[k], k)
        return total + self.x(total)


def plus(left, right):
    return (left.astype(F32) + right.astype(F32)).astype(BF16)


def place_tables(depth, narrow):
    wide = 4 * depth
    found = np.zeros((wide * narrow, 168), np.int32)
    for z0 in range(depth):
        for y0 in range(2):
            for c0 in range(2):
                for x0 in range(narrow):
                    row = found[((z0 * 2 + y0) * 2 + c0) * narrow + x0]
                    for p in range(2 * PIECES):
                        dc, h, a, b, k = p // 32, p // 16 % 2, p // 8 % 2, p // 4 % 2, p % 4
                        dx, dy = (a, b) if h == 0 else (b, a)
                        chunk = 2 * h + (x0 ^ dx)
                        w = (((z0 - k) % depth) * 2 + (y0 ^ dy)) * 2 + (c0 ^ dc)
                        row[p] = chunk * wide + w
                        row[64 + p] = w * 4 + chunk
                    for chunk in range(4):
                        for z in range(depth):
                            for y in range(2):
                                k, dx, dy = (z - z0) % depth, x0 ^ (chunk & 1), y0 ^ y
                                at = dx * 8 + dy * 4 if chunk < 2 else 16 + dy * 8 + dx * 4
                                row[128 + chunk * 8 + z * 2 + y] = at + k
                    row[160] = c0
    return found


def order_tables(depth):
    wide = 4 * depth
    arrive_in = np.zeros((wide, wide, wide), np.float32)
    leave_in = np.zeros((wide, wide, wide), np.float32)
    for own in range(wide):
        z0, y0, c0 = own // 4, own // 2 % 2, own % 2
        for dc in range(2):
            for dy in range(2):
                for k in range(depth):
                    at = (dc * 2 + dy) * depth + k
                    low = (y0 ^ dy) * 2 + (c0 ^ dc)
                    arrive_in[own, ((z0 - k) % depth) * 4 + low, at] = 1
                    leave_in[own, at, ((z0 + k) % depth) * 4 + low] = 1
    return arrive_in, leave_in


def body(
    mesh_shape,
    tokens, qkv_weight, qv_bias, proj_weight, proj_bias, fc1_weight, fc1_bias, fc2_weight,
    fc2_bias, norm1_gain, norm1_shift, norm2_gain, norm2_shift, segment_ids, key_mask,
    positions, cotangent,
):
    wide, narrow = mesh_shape["wide"], mesh_shape["narrow"]
    part = D // wide
    by_hops = part == BLOCK and narrow == 2
    ring = Ring(mesh_shape)
    here = lax.axis_index("wide")
    x_here = lax.axis_index("narrow")
    small_mine = jnp.concatenate(
        [
            qv_bias.reshape(-1), proj_bias, fc2_bias, norm1_gain, norm1_shift, norm2_gain,
            norm2_shift, fc1_bias,
        ]
    ).astype(F32)

    def columns(weight):
        return [weight[:, j * D : (j + 1) * D] for j in range(weight.shape[1] // D)]

    shards = (
        columns(qkv_weight) + [proj_weight],
        columns(fc1_weight),
        [fc2_weight[q * part : (q + 1) * part] for q in range(4)],
    )
    if by_hops:
        tables = jnp.asarray(place_tables(wide // 4, narrow))
        tab = lax.dynamic_index_in_dim(tables, here * narrow + x_here, 0, keepdims=False)
        arrive_in, leave_in = order_tables(wide // 4)
    else:
        tab = jnp.concatenate(
            [jnp.arange(128, dtype=jnp.int32) % 64, jnp.arange(32, dtype=jnp.int32),
             jnp.zeros((8,), jnp.int32)]
        )

    def vec_of():
        if by_hops:
            arrived = ring.gather_small(small_mine)
            turn = lax.dynamic_index_in_dim(jnp.asarray(arrive_in), here, 0, keepdims=False)
            arrived = jnp.dot(turn, arrived, precision=lax.Precision.HIGHEST)
        else:
            arrived = lax.all_gather(small_mine, "wide", axis=0)
        rows = arrived[:, : 8 * part].reshape(wide, 8, part).transpose(1, 0, 2).reshape(8, D)
        return jnp.concatenate([rows, arrived[:, 8 * part :].reshape(4, D)], axis=0)

    def groups(i):
        chunks = shards[i]
        if by_hops:
            odd = x_here == 1
            mine = jnp.stack(
                [jnp.where(odd, chunks[1], chunks[0]), jnp.where(odd, chunks[3], chunks[2])]
            )
            own, other = ring.gather(mine)
            return own.reshape(PIECES, BLOCK, D), other.reshape(PIECES, BLOCK, D)
        full = lax.all_gather(jnp.stack(chunks), "wide", axis=0)
        if i < 2:
            full = full.transpose(1, 0, 2, 3)
        full = full.reshape(2 * PIECES, BLOCK, D)
        return full[:PIECES], full[PIECES:]

    def spread(i, own, send):
        if by_hops:
            total, other = ring.scatter(own, send)
            odd = x_here == 1
            return [
                jnp.where(odd, other[0], total[0]), jnp.where(odd, total[0], other[0]),
                jnp.where(odd, other[1], total[1]), jnp.where(odd, total[1], other[1]),
            ]
        full = jnp.stack([own, send], axis=1).reshape(4, 8, 2 * BLOCK, D)
        if i == 2:
            full = full.reshape(4, 8, 2, BLOCK, D).transpose(1, 2, 0, 3, 4)
            full = full.reshape(wide, 4, part, D)
        else:
            full = full.reshape(4, wide, part, D).transpose(1, 0, 2, 3)
        full = lax.psum_scatter(full.astype(F32), "wide", scatter_dimension=0)
        full = lax.psum(full, "narrow")
        return [full[j] for j in range(4)]

    block_out, grad_tokens, done_q, done_u, done_d, small = compute(
        tab, vec_of, tokens, segment_ids, key_mask, positions, cotangent, groups, spread
    )
    small = jnp.concatenate(
        [
            small[0].reshape(8, wide, part).transpose(1, 0, 2).reshape(wide, 8 * part),
            small[1].reshape(wide, 4 * part),
        ],
        axis=1,
    )
    if by_hops:
        turn = lax.dynamic_index_in_dim(jnp.asarray(leave_in), here, 0, keepdims=False)
        small = ring.scatter_small(jnp.dot(turn, small, precision=lax.Precision.HIGHEST))
    else:
        small = lax.psum(
            lax.psum_scatter(small, "wide", scatter_dimension=0, tiled=True)[0], "narrow"
        )
    line = lambda i: small[i * part : (i + 1) * part]
    return (
        block_out,
        grad_tokens,
        jnp.concatenate(done_q[:3], axis=1),
        jnp.stack([line(0), line(1)]),
        done_q[3],
        line(2),
        jnp.concatenate(done_u, axis=1),
        small[8 * part :],
        jnp.concatenate(done_d, axis=0),
        line(3),
        line(4),
        line(5),
        line(6),
        line(7),
    )


def solution(mesh):
    both = ("wide", "narrow")
    row = P("wide", None)
    one = P("wide")
    placed = (
        P(both, None), row, P(None, "wide"), row, one, row, one, row,
        one, one, one, one, one, P(both), P(both), P(both), P(both, None),
    )
    return jax.shard_map(
        partial(body, dict(mesh.shape)),
        mesh=mesh,
        in_specs=placed,
        out_specs=(
            P(both, None), P(both, None), row, P(None, "wide"), row, one, row, one, row,
            one, one, one, one, one,
        ),
        check_vma=False,
    )
```
